32 devices in a mesh: tm: 4 (over z), dp: 8 (over y, x, core).
Axes of the slice: x: 2, y: 2, z: 4, core: 2. Of those that a mesh axis runs over, the one named last changes fastest.
Arguments:
- loaded: bfloat16 [8, 32, 8, 16, 128], P('dp', 'tm'), may hold values from -6 to 6
- frame_index: int32 [8, 32], P('dp', 'tm'), may hold values from 0 to 31, as said below
- out_grad: bfloat16 [8, 32, 8, 16, 128], P('dp', 'tm'), may hold values from -6 to 6
- kernel: bfloat16 [3, 3, 3, 128, 128], replicated, may hold values from -0.109375 to 0.109375
- conv_bias: float32 [128], replicated, may hold values from -3 to 3
Outputs:
- activated: bfloat16 [8, 32, 8, 16, 128], P('dp', 'tm')
- input_grad: bfloat16 [8, 32, 8, 16, 128], P('dp', 'tm')
- kernel_grad: float32 [3, 3, 3, 128, 128], replicated
- bias_grad: float32 [128], replicated
The draws below stay inside these ranges and needn't reach their ends.
Inputs may be any that keep to these rules, and one draw needn't show every extreme that they name: Each clip's row of frame_index holds every frame number once. Loader row r lies on loader shard r // 8, frame f belongs to owner f // 8; at most 3 rows of one loader shard belong to one owner, and in every clip every loader shard sends exactly 3 rows to one owner.
All inputs are finite; a program needn't handle non-finite values.
Results may differ from the reference program's by a relative error of at most 0.005.
Values may be sent and summed in bfloat16 or wider, within the bound.
A program may use at most 64 MiB of HBM per device.

```python
import math
import jax
import jax.numpy as jnp
from jax import lax

C = 128
TILE_H = 8
TILE_W = 16
F_DEV = 8
CAP = 3
CLIPS = 8
FRAMES = 32
CELLS = 32768


def draw_frame_index(key, part):
    shards = FRAMES // F_DEV
    base_key = jax.random.fold_in(key, 11)
    first_key, second_key, third_key = jax.random.split(base_key, 3)
    shift_of = jax.random.randint(first_key, (CLIPS, 1), 0, shards)
    spread = jax.random.randint(second_key, (CLIPS, 1), 0, shards - 1)
    group_ids = jnp.arange(F_DEV)[None, :]
    extra = jnp.maximum(group_ids - CAP, 0)
    offsets = jnp.where(group_ids < CAP, shift_of, shift_of + 1 + (extra + spread) % (shards - 1)) % shards
    sources = jnp.arange(shards)
    owners = (sources[None, :, None] + offsets[:, None, :]) % shards
    sub_keys = jax.random.split(third_key, CLIPS * shards)
    shuffles = jax.vmap(lambda one_key: jax.random.permutation(one_key, F_DEV))(sub_keys).reshape(CLIPS, shards, F_DEV)
    clip_ids = jnp.arange(CLIPS)[:, None, None]
    slots = shuffles[clip_ids, owners, group_ids[None, :, :] + 0 * owners]
    frame_ids = owners * F_DEV + slots
    return frame_ids.reshape(CLIPS, FRAMES).astype(jnp.int32)


def steps_of(own_key, dims, cuts, least, largest):
    gain = 1.0
    for axis_at, shards_of in cuts:
        heights = jax.random.uniform(jax.random.fold_in(jax.random.fold_in(own_key, 6), axis_at), (shards_of,), jnp.float32, least / len(cuts), largest / len(cuts))
        gain = gain * jnp.repeat(jnp.exp(heights), dims[axis_at] // shards_of).reshape((-1,) + (1,) * (len(dims) - 1 - axis_at))
    return gain


def noise(key, dims, scale, bound, cuts=(), dtype=jnp.bfloat16):
    drawn = scale * jax.random.normal(key, dims, jnp.float32)
    if cuts:
        drawn = drawn * steps_of(key, dims, cuts, -0.22, 0.18)
    return jnp.clip(drawn, -bound, bound).astype(dtype)


def setup_inputs(seed: int = 0) -> dict:
    seeds = jax.random.split(jax.random.key(seed), 6)
    return {
        "loaded": noise(seeds[0], (CLIPS, FRAMES, TILE_H, TILE_W, C), 1.0, 6.0, ((0, 8), (1, 4))),
        "frame_index": draw_frame_index(jax.random.fold_in(seeds[5], 71), 0),
        "out_grad": noise(seeds[2], (CLIPS, FRAMES, TILE_H, TILE_W, C), 1.0, 6.0, ((0, 8), (1, 4))),
        "kernel": noise(seeds[3], (3, 3, 3, C, C), (27 * C) ** -0.5, 0.109375),
        "conv_bias": noise(seeds[4], (C,), 0.5, 3.0, (), jnp.float32),
    }


def stack_taps(padded, frame_count, tile_h, tile_w, starts):
    pieces = [padded[lag_off:lag_off + frame_count, row_off:row_off + tile_h, col_off:col_off + tile_w] for lag_off, row_off, col_off in starts]
    stacked = jnp.stack(pieces, axis=3)
    return stacked.reshape(frame_count * tile_h * tile_w, -1)

def one_clip(loaded_clip, index_clip, grad_clip, kernel, conv_bias):
    chans = loaded_clip.shape[-1]
    frames = jnp.zeros_like(loaded_clip).at[index_clip].set(loaded_clip)
    forward_starts = [(p, q, s) for p in range(3) for q in range(3) for s in range(3)]
    backward_starts = [(2 - p, 2 - q, 2 - s) for p in range(3) for q in range(3) for s in range(3)]
    padded = jnp.pad(frames, ((2, 0), (1, 1), (1, 1), (0, 0)))
    patches = stack_taps(padded, FRAMES, TILE_H, TILE_W, forward_starts)
    preact = jnp.dot(patches, kernel.reshape(27 * chans, chans), preferred_element_type=jnp.float32) + conv_bias[None, :]
    sigma = jax.nn.sigmoid(preact)
    activated = (preact * sigma).astype(jnp.bfloat16)
    gate_grad = (grad_clip.reshape(-1, chans).astype(jnp.float32) * sigma * (1.0 + preact * (1.0 - sigma))).astype(jnp.bfloat16)
    gate_pad = jnp.pad(gate_grad.reshape(FRAMES, TILE_H, TILE_W, chans), ((0, 2), (1, 1), (1, 1), (0, 0)))
    back_patches = stack_taps(gate_pad, FRAMES, TILE_H, TILE_W, backward_starts)
    back_kernel = jnp.transpose(kernel, (0, 1, 2, 4, 3)).reshape(27 * chans, chans)
    input_grad = jnp.dot(back_patches, back_kernel, preferred_element_type=jnp.float32).astype(jnp.bfloat16)
    kernel_term = lax.dot_general(patches, gate_grad, (((0,), (0,)), ((), ())), preferred_element_type=jnp.float32)
    bias_term = lax.optimization_barrier(jnp.sum(gate_grad.astype(jnp.float32), axis=0))
    shape = (FRAMES, TILE_H, TILE_W, chans)
    return (activated.reshape(shape), input_grad.reshape(shape), kernel_term, bias_term)

def reference(loaded, frame_index, out_grad, kernel, conv_bias):
    chans = loaded.shape[-1]

    def step(carry, inputs):
        loaded_clip, index_clip, grad_clip = inputs
        activated, input_grad, kernel_term, bias_term = one_clip(loaded_clip, index_clip.astype(jnp.int32), grad_clip, kernel, conv_bias)
        return ((carry[0] + kernel_term, carry[1] + bias_term), (activated, input_grad))
    start = (jnp.zeros((27 * chans, chans), jnp.float32), jnp.zeros((chans,), jnp.float32))
    totals, outputs = lax.scan(step, start, (loaded, frame_index, out_grad))
    scale = 1.0 / math.sqrt(CELLS)
    kernel_grad = (totals[0] * scale).reshape(3, 3, 3, chans, chans)
    bias_grad = totals[1] * scale
    return (outputs[0], outputs[1], kernel_grad, bias_grad)
```

```python
import functools
import math

import jax
import jax.numpy as jnp
from jax import lax
from jax.experimental import pallas as pl
from jax.experimental.pallas import tpu as pltpu
from jax.sharding import PartitionSpec as P

CAP = 3
F32, BF16 = jnp.float32, jnp.bfloat16


def each(first, last, step):
    if last - first <= 4:
        for i in range(first, last):
            step(i)
    else:
        lax.fori_loop(first, last, lambda i, carry: (step(i), carry)[1], 0)


def kernel_body(
    dims, ids, loaded, og_hbm, w_hbm, bias,
    act, igrad, total, bgrad,
    og, w, wt, slots, rslots, frames, xc, xt, gc, dwf, dwb,
    pair_in, s32, s16, xy_in, z32, z16, z_in, b_own, b_pair, bx, bz,
    ld_sem, f_s, f_r, h_s, h_r, g_s, g_r, p_s, p_r, x_s, x_r, zs_s, zs_r,
    az_s, az_r, ax_s, ax_r, ap_s, ap_r, bp_s, bp_r, bx_s, bx_r, bz_s, bz_r,
):
    T, D, F, H, W, C, R, U = dims
    Q = D // 2
    HW = H * W
    K3 = 3 * C
    z = lax.axis_index("tm")
    dp = lax.axis_index("dp")
    c, q = dp % 2, dp // 2

    def at(tm=None, chip=None, core=None):
        return {
            "tm": z if tm is None else tm,
            "dp": (q if chip is None else chip) * 2 + (c if core is None else core),
        }

    def to_z(k):
        return at(tm=(z + k) % T)

    def to_q(k):
        return at(chip=(q + k) % Q)

    other = at(core=1 - c)

    def remote(src, dst, ss, rs, where):
        return pltpu.make_async_remote_copy(
            src_ref=src, dst_ref=dst, send_sem=ss, recv_sem=rs,
            device_id=where, device_id_type=pl.DeviceIdType.MESH,
        )

    load_w = pltpu.make_async_copy(w_hbm, w, ld_sem.at[0])
    load_og = pltpu.make_async_copy(og_hbm, og, ld_sem.at[1])
    load_w.start()
    load_og.start()

    barrier = pltpu.get_barrier_semaphore()

    def greet(where):
        pl.semaphore_signal(barrier, 1, device_id=where, device_id_type=pl.DeviceIdType.MESH)

    greet(other)
    each(1, Q, lambda k: greet(to_q(k)))
    each(1, T, lambda k: greet(to_z(k)))

    owners = [ids[0, r] // F for r in range(F)]
    rank = []
    for r in range(F):
        before = jnp.int32(0)
        for s in range(r):
            before = before + jnp.where(owners[s] == owners[r], 1, 0)
        rank.append(before)

    def pack(k):
        owner = (z + k) % T
        for s in range(CAP):
            row, target = jnp.int32(0), jnp.int32(-1)
            for r in range(F):
                hit = jnp.logical_and(owners[r] == owner, rank[r] == s)
                row = jnp.where(hit, r, row)
                target = jnp.where(hit, ids[0, r] - owner * F, target)
            slots[k, s, 0:H] = loaded[row]
            slots[k, s, H] = jnp.full((W, C), target.astype(F32), F32).astype(BF16)

    each(0, T, pack)
    pl.semaphore_wait(barrier, 1 + (Q - 1) + (T - 1))

    def row_copy(k):
        return remote(slots.at[k], rslots.at[k], f_s.at[k], f_r.at[k], to_z(k))

    each(1, T, lambda k: row_copy(k).start())

    for e in range(F + 2):
        for ref in (xc, gc):
            ref[e, 0] = jnp.zeros((W, K3), BF16)
            ref[e, H + 1] = jnp.zeros((W, K3), BF16)
    taps_rows = 3 * K3
    if D * R > taps_rows:
        for a in range(3):
            dwf[a, taps_rows:] = jnp.zeros((D * R - taps_rows, C), F32)
            dwb[a, taps_rows:] = jnp.zeros((D * R - taps_rows, C), BF16)
    if T * U > 3 * R:
        z32[3 * R :] = jnp.zeros((T * U - 3 * R, C), F32)
        z16[3 * R :] = jnp.zeros((T * U - 3 * R, C), BF16)
    load_w.wait()
    for p in range(9):
        for j in range(3):
            wt[p, j * C : (j + 1) * C, :] = w[p, j * C : (j + 1) * C, :].T
    load_og.wait()

    each(1, T, lambda k: row_copy(k).wait_recv())

    def place(f):
        picked = jnp.zeros((H, W, C), BF16)
        for k in range(T):
            source = slots if k == 0 else rslots
            for s in range(CAP):
                gap = jnp.abs(source[k, s, H] - jnp.asarray(f, BF16))
                weight = jnp.maximum(jnp.asarray(1, BF16) - gap, jnp.asarray(0, BF16))
                picked = picked + source[k, s, 0:H] * weight[None]
        frames[f + 2] = picked

    for f in (F - 2, F - 1):
        place(f)

    def halo_copy():
        return remote(frames.at[pl.ds(F, 2)], frames.at[pl.ds(0, 2)], h_s, h_r, to_z(1))

    def gate_copy():
        return remote(
            gate_out, gate_in, g_s, g_r, to_z(T - 1)
        )

    @pl.when(z < T - 1)
    def _():
        halo_copy().start()

    for f in range(F - 2):
        place(f)

    column = lax.broadcasted_iota(jnp.int32, (HW, C), 0) % W

    def shifted(value):
        left = jnp.where(column == 0, 0.0, pltpu.roll(value, 1, 0))
        right = jnp.where(column == W - 1, 0.0, pltpu.roll(value, HW - 1, 0))
        return left.astype(BF16), right.astype(BF16)

    def spread(e):
        mid = frames[e].reshape(HW, C)
        left, right = shifted(mid.astype(F32))
        for j, part in enumerate((left, mid, right)):
            xc[e, 1 : H + 1, :, j * C : (j + 1) * C] = part.reshape(H, W, C)
            xt[j * C : (j + 1) * C, e * HW : (e + 1) * HW] = part.T

    for e in range(2, F + 2):
        spread(e)

    def forward(t, n):
        pre = jnp.broadcast_to(bias[...], (n * HW, C))
        for a in range(3):
            for i in range(3):
                rows = xc[t + a : t + a + n, i : i + H].reshape(n * HW, K3)
                pre = pre + jnp.dot(rows, w[a * 3 + i], preferred_element_type=F32)
        sigma = jax.nn.sigmoid(pre)
        act[t : t + n] = (pre * sigma).astype(BF16).reshape(n, H, W, C)
        cot = og[t : t + n].reshape(n * HW, C).astype(F32)
        gate = (cot * sigma * (1.0 + pre * (1.0 - sigma))).astype(BF16)
        gc[t : t + n, 1 : H + 1, :, C : 2 * C] = gate.reshape(n, H, W, C)
        return jnp.sum(gate.astype(F32).reshape(n * HW // 8, 8, C), axis=0)

    bias_sum = jnp.zeros((8, C), F32)
    for t in range(2, F, 2):
        bias_sum = bias_sum + forward(t, 2)

    @pl.when(z > 0)
    def _():
        halo_copy().wait_recv()

    @pl.when(z == 0)
    def _():
        frames[0:2] = jnp.zeros((2, H, W, C), BF16)

    for e in range(2):
        spread(e)
    bias_sum = bias_sum + forward(0, 2)
    b_own[...] = bias_sum

    gate_out, gate_in = frames.at[pl.ds(F + 2, 2)], frames.at[pl.ds(F + 4, 2)]
    for t in range(2):
        frames[F + 2 + t] = gc[t, 1 : H + 1, :, C : 2 * C]

    @pl.when(z > 0)
    def _():
        gate_copy().start()

    half = Q * R

    def my_half(core):
        return pl.ds(pl.multiple_of(core * half, 16), half)

    def pair_copy(a):
        return remote(dwb.at[a, my_half(1 - c)], pair_in.at[a], p_s.at[a], p_r.at[a], other)

    def xy_copy(a, k):
        there = pl.ds(pl.multiple_of(((q + k) % Q) * R, 16), R)
        return remote(
            s16.at[a, there], xy_in.at[a, k], x_s.at[a, k], x_r.at[a, k], to_q(k)
        )

    def z_copy(k):
        there = pl.ds(pl.multiple_of(((z + k) % T) * U, 16), U)
        return remote(z16.at[there], z_in.at[k], zs_s.at[k], zs_r.at[k], to_z(k))

    def bias_pair():
        return remote(b_own, b_pair, bp_s, bp_r, other)

    def bias_q(k):
        return remote(bx.at[q], bx.at[q], bx_s.at[k], bx_r.at[k], to_q(k))

    def bias_z(k):
        return remote(bz.at[z], bz.at[z], bz_s.at[k], bz_r.at[k], to_z(k))

    def weight_term(a):
        gates = jnp.concatenate(
            [
                gc[0:F, 2 - i : 2 - i + H, :, C : 2 * C].reshape(F * HW, C)
                for i in range(3)
            ],
            axis=1,
        )
        term = jnp.dot(xt[:, a * HW : (a + F) * HW], gates, preferred_element_type=F32)
        for i in range(3):
            block = term[:, i * C : (i + 1) * C]
            dwf[a, i * K3 : (i + 1) * K3] = block
            dwb[a, i * K3 : (i + 1) * K3] = block.astype(BF16)

    def after_pair(a):
        pair_copy(a).wait_recv()
        both = dwf[a, my_half(c)] + pair_in[a].astype(F32)
        s32[a] = both
        s16[a] = both.astype(BF16)
        each(1, Q, lambda k: xy_copy(a, k).start())

    bias_pair().start()
    weight_term(0)
    pair_copy(0).start()
    weight_term(1)
    pair_copy(1).start()
    after_pair(0)
    weight_term(2)
    pair_copy(2).start()
    after_pair(1)
    bias_pair().wait_recv()
    bx[q] = b_own[...] + b_pair[...]
    each(1, Q, lambda k: bias_q(k).start())

    def spread_gate(t, mid):
        left, right = shifted(mid.astype(F32))
        gc[t, 1 : H + 1, :, 0:C] = right.reshape(H, W, C)
        gc[t, 1 : H + 1, :, 2 * C :] = left.reshape(H, W, C)

    for t in range(F):
        spread_gate(t, gc[t, 1 : H + 1, :, C : 2 * C].reshape(HW, C))
    after_pair(2)

    def backward(t, n):
        out = jnp.zeros((n * HW, C), F32)
        for a in range(3):
            for i in range(3):
                rows = gc[t + 2 - a : t + 2 - a + n, 2 - i : 2 - i + H].reshape(n * HW, K3)
                out = out + jnp.dot(rows, wt[a * 3 + i], preferred_element_type=F32)
        igrad[t : t + n] = out.astype(BF16).reshape(n, H, W, C)

    backward(0, 2)
    backward(2, 2)

    def after_xy(a):
        here = pl.ds(pl.multiple_of(q * R, 16), R)
        each(1, Q, lambda k: xy_copy(a, k).wait_recv())
        got = s32[a, here]
        for k in range(1, Q):
            got = got + xy_in[a, k].astype(F32)
        z32[a * R : (a + 1) * R] = got
        z16[a * R : (a + 1) * R] = got.astype(BF16)

    for a in range(3):
        after_xy(a)
    each(1, T, lambda k: z_copy(k).start())
    each(1, Q, lambda k: bias_q(k).wait_recv())
    got = bx[0]
    for k in range(1, Q):
        got = got + bx[k]
    bz[z] = got
    each(1, T, lambda k: bias_z(k).start())

    backward(4, 2)

    each(1, T, lambda k: z_copy(k).wait_recv())
    got = z32[pl.ds(pl.multiple_of(z * U, 16), U)]
    for k in range(1, T):
        got = got + z_in[k].astype(F32)
    block = c * Q + q
    total[block, z] = got.astype(BF16)

    def piece(k, kz):
        return total.at[c * Q + (q + Q - k) % Q, (z + T - kz) % T]

    def gather_z(k):
        return remote(piece(0, 0), piece(0, 0), az_s.at[k], az_r.at[k], to_z(k))

    def gather_q(kz, k):
        return remote(piece(0, kz), piece(0, kz), ax_s.at[kz, k], ax_r.at[kz, k], to_q(k))

    def gather_pair(kz, k):
        return remote(piece(k, kz), piece(k, kz), ap_s.at[kz, k], ap_r.at[kz, k], other)

    def send_on(kz):
        each(1, Q, lambda k: gather_q(kz, k).start())
        gather_pair(kz, 0).start()

    each(1, T, lambda k: gather_z(k).start())
    send_on(0)

    @pl.when(z < T - 1)
    def _():
        gate_copy().wait_recv()

    @pl.when(z == T - 1)
    def _():
        frames[F + 4 : F + 6] = jnp.zeros((2, H, W, C), BF16)

    for t in range(2):
        mid = frames[F + 4 + t]
        gc[F + t, 1 : H + 1, :, C : 2 * C] = mid
        spread_gate(F + t, mid.reshape(HW, C))

    def relay_z(kz):
        gather_z(kz).wait_recv()
        send_on(kz)

    def relay_q(kz):
        def one(k):
            gather_q(kz, k).wait_recv()
            gather_pair(kz, k).start()

        each(1, Q, one)

    each(1, T, relay_z)
    backward(6, 2)
    each(0, T, relay_q)

    each(1, T, lambda k: bias_z(k).wait_recv())
    got = bz[0]
    for k in range(1, T):
        got = got + bz[k]
    bgrad[...] = jnp.sum(got, axis=0, keepdims=True)

    each(0, T, lambda kz: each(0, Q, lambda k: gather_pair(kz, k).wait_recv()))

    each(1, T, lambda k: row_copy(k).wait_send())

    @pl.when(z < T - 1)
    def _():
        halo_copy().wait_send()

    @pl.when(z > 0)
    def _():
        gate_copy().wait_send()

    bias_pair().wait_send()
    each(1, Q, lambda k: bias_q(k).wait_send())
    each(1, T, lambda k: bias_z(k).wait_send())
    for a in range(3):
        pair_copy(a).wait_send()
        each(1, Q, lambda k: xy_copy(a, k).wait_send())
    each(1, T, lambda k: z_copy(k).wait_send())
    each(1, T, lambda k: gather_z(k).wait_send())
    each(0, T, lambda kz: each(1, Q, lambda k: gather_q(kz, k).wait_send()))
    each(0, T, lambda kz: each(0, Q, lambda k: gather_pair(kz, k).wait_send()))


def body(T, D, loaded, frame_index, out_grad, kernel, conv_bias):
    _, F, H, W, C = loaded.shape
    Q = D // 2
    K3, HW = 3 * C, H * W
    R = 16 * pl.cdiv(pl.cdiv(3 * K3, 16), D)
    U = 16 * pl.cdiv(3 * R // 16, T)
    dims = (T, D, F, H, W, C, R, U)
    vmem = pl.BlockSpec(memory_space=pltpu.VMEM)
    hbm = pl.BlockSpec(memory_space=pl.ANY)
    V = pltpu.VMEM
    S = pltpu.SemaphoreType.DMA
    act, igrad, total, bgrad = pl.pallas_call(
        functools.partial(kernel_body, dims),
        out_shape=(
            jax.ShapeDtypeStruct((F, H, W, C), BF16),
            jax.ShapeDtypeStruct((F, H, W, C), BF16),
            jax.ShapeDtypeStruct((D, T, U, C), BF16),
            jax.ShapeDtypeStruct((1, C), F32),
        ),
        in_specs=[pl.BlockSpec(memory_space=pltpu.SMEM), vmem, hbm, hbm, vmem],
        out_specs=(vmem, vmem, vmem, vmem),
        scratch_shapes=[
            V((F, H, W, C), BF16), V((9, K3, C), BF16), V((9, K3, C), BF16),
            V((T, CAP, H + 1, W, C), BF16), V((T, CAP, H + 1, W, C), BF16),
            V((F + 6, H, W, C), BF16),
            V((F + 2, H + 2, W, K3), BF16), V((K3, (F + 2) * HW), BF16),
            V((F + 2, H + 2, W, K3), BF16),
            V((3, D * R, C), F32), V((3, D * R, C), BF16),
            V((3, Q * R, C), BF16), V((3, Q * R, C), F32), V((3, Q * R, C), BF16),
            V((3, Q, R, C), BF16), V((T * U, C), F32), V((T * U, C), BF16),
            V((T, U, C), BF16),
            V((8, C), F32), V((8, C), F32), V((Q, 8, C), F32), V((T, 8, C), F32),
            S((2,)), S((T,)), S((T,)), S, S, S, S,
            S((3,)), S((3,)), S((3, Q)), S((3, Q)), S((T,)), S((T,)),
            S((T,)), S((T,)), S((T, Q)), S((T, Q)), S((T, Q)), S((T, Q)),
            S, S, S((Q,)), S((Q,)), S((T,)), S((T,)),
        ],
        compiler_params=pltpu.CompilerParams(
            collective_id=0, has_side_effects=True, vmem_limit_bytes=48 * 1024 * 1024
        ),
    )(frame_index, loaded[0], out_grad[0], kernel.reshape(9, K3, C), conv_bias[None])
    scale = 1.0 / math.sqrt(T * F * HW * D * loaded.shape[0])
    rows = total.reshape(D, T * U, C)[:, : 3 * R].reshape(D, 3, R, C)
    rows = jnp.swapaxes(rows, 0, 1).reshape(3, D * R, C)[:, : 3 * K3]
    kernel_grad = (rows.astype(F32) * scale).reshape(kernel.shape)
    return act[None], igrad[None], kernel_grad, bgrad[0] * scale


def solution(mesh):
    spread = P("dp", "tm", None, None, None)
    return jax.shard_map(
        functools.partial(body, mesh.shape["tm"], mesh.shape["dp"]),
        mesh=mesh,
        in_specs=(spread, P("dp", "tm"), spread, P(), P()),
        out_specs=(spread, spread, P(), P()),
        check_vma=False,
    )
```

```python
import functools
import math

import jax
import jax.numpy as jnp
from jax import lax
from jax.experimental import pallas as pl
from jax.experimental.pallas import tpu as pltpu
from jax.sharding import PartitionSpec as P

CAP = 3
F32, BF16 = jnp.float32, jnp.bfloat16


def each(first, last, step):
    if last - first <= 4:
        for i in range(first, last):
            step(i)
    else:
        lax.fori_loop(first, last, lambda i, carry: (step(i), carry)[1], 0)


def kernel_body(
    dims, ids_hbm, loaded_hbm, og_hbm, w_hbm, bias_hbm,
    act, igrad, total, bgrad,
    ids, loaded, bias, og, w, wt, slots, rslots, frames, xc, xt, gc, dwf, dwb,
    pair_in, s32, s16, xy_in, z32, z16, z_in, b_own, b_pair, bx, bz,
    ld_sem, f_s, f_r, h_s, h_r, g_s, g_r, p_s, p_r, x_s, x_r, zs_s, zs_r,
    az_s, az_r, ax_s, ax_r, ap_s, ap_r, bp_s, bp_r, bx_s, bx_r, bz_s, bz_r,
):
    T, D, F, H, W, C, R, U = dims
    Q = D // 2
    HW = H * W
    K3 = 3 * C
    z = lax.axis_index("tm")
    dp = lax.axis_index("dp")
    c, q = dp % 2, dp // 2

    def at(tm=None, chip=None, core=None):
        return {
            "tm": z if tm is None else tm,
            "dp": (q if chip is None else chip) * 2 + (c if core is None else core),
        }

    def to_z(k):
        return at(tm=(z + k) % T)

    def to_q(k):
        return at(chip=(q + k) % Q)

    other = at(core=1 - c)

    def remote(src, dst, ss, rs, where):
        return pltpu.make_async_remote_copy(
            src_ref=src, dst_ref=dst, send_sem=ss, recv_sem=rs,
            device_id=where, device_id_type=pl.DeviceIdType.MESH,
        )

    loads = [
        pltpu.make_async_copy(source, target, ld_sem.at[n])
        for n, (source, target) in enumerate(
            [(ids_hbm, ids), (loaded_hbm, loaded), (w_hbm, w), (og_hbm, og), (bias_hbm, bias)]
        )
    ]
    for load in loads:
        load.start()

    barrier = pltpu.get_barrier_semaphore()

    def greet(where):
        pl.semaphore_signal(barrier, 1, device_id=where, device_id_type=pl.DeviceIdType.MESH)

    greet(other)
    each(1, Q, lambda k: greet(to_q(k)))
    each(1, T, lambda k: greet(to_z(k)))

    loads[0].wait()
    loads[1].wait()

    owners = [ids[0, r] // F for r in range(F)]
    rank = []
    for r in range(F):
        before = jnp.int32(0)
        for s in range(r):
            before = before + jnp.where(owners[s] == owners[r], 1, 0)
        rank.append(before)

    line = lax.broadcasted_iota(jnp.int32, (W, C), 0)

    def pack(k):
        owner = (z + k) % T
        targets = jnp.zeros((W, C), F32)
        for s in range(CAP):
            row, target = jnp.int32(0), jnp.int32(-1)
            for r in range(F):
                hit = jnp.logical_and(owners[r] == owner, rank[r] == s)
                row = jnp.where(hit, r, row)
                target = jnp.where(hit, ids[0, r] - owner * F, target)
            slots[k, s * H : (s + 1) * H] = loaded[row]
            targets = jnp.where(line == s, target.astype(F32), targets)
        slots[k, CAP * H] = targets.astype(BF16)

    each(0, T, pack)
    pl.semaphore_wait(barrier, 1 + (Q - 1) + (T - 1))

    def row_copy(k):
        return remote(slots.at[k], rslots.at[k], f_s.at[k], f_r.at[k], to_z(k))

    each(1, T, lambda k: row_copy(k).start())

    for e in range(F + 2):
        for ref in (xc, gc):
            ref[e, 0] = jnp.zeros((W, K3), BF16)
            ref[e, H + 1] = jnp.zeros((W, K3), BF16)
    taps_rows = 3 * K3
    if D * R > taps_rows:
        for a in range(3):
            dwf[a, taps_rows:] = jnp.zeros((D * R - taps_rows, C), F32)
            dwb[a, taps_rows:] = jnp.zeros((D * R - taps_rows, C), BF16)
    if T * U > 3 * R:
        z32[3 * R :] = jnp.zeros((T * U - 3 * R, C), F32)
        z16[3 * R :] = jnp.zeros((T * U - 3 * R, C), BF16)
    loads[2].wait()
    for p in range(9):
        for j in range(3):
            wt[p, j * C : (j + 1) * C, :] = w[p, j * C : (j + 1) * C, :].T
    loads[3].wait()
    loads[4].wait()

    each(1, T, lambda k: row_copy(k).wait_recv())

    def place(f):
        picked = jnp.zeros((H, W, C), BF16)
        for k in range(T):
            source = slots if k == 0 else rslots
            for s in range(CAP):
                gap = jnp.abs(source[k, CAP * H, s : s + 1].astype(F32) - f)
                weight = jnp.broadcast_to(jnp.maximum(1.0 - gap, 0.0), (W, C)).astype(BF16)
                picked = picked + source[k, s * H : (s + 1) * H] * weight[None]
        frames[f + 2] = picked

    for f in (F - 2, F - 1):
        place(f)

    def halo_copy():
        return remote(frames.at[pl.ds(F, 2)], frames.at[pl.ds(0, 2)], h_s, h_r, to_z(1))

    def gate_copy():
        return remote(
            gate_out, gate_in, g_s, g_r, to_z(T - 1)
        )

    @pl.when(z < T - 1)
    def _():
        halo_copy().start()

    for f in range(F - 2):
        place(f)

    column = lax.broadcasted_iota(jnp.int32, (HW, C), 0) % W

    def shifted(value):
        left = jnp.where(column == 0, 0.0, pltpu.roll(value, 1, 0))
        right = jnp.where(column == W - 1, 0.0, pltpu.roll(value, HW - 1, 0))
        return left.astype(BF16), right.astype(BF16)

    def spread(e):
        mid = frames[e].reshape(HW, C)
        left, right = shifted(mid.astype(F32))
        for j, part in enumerate((left, mid, right)):
            xc[e, 1 : H + 1, :, j * C : (j + 1) * C] = part.reshape(H, W, C)
            xt[j * C : (j + 1) * C, e * HW : (e + 1) * HW] = part.T

    for e in range(2, F + 2):
        spread(e)

    def forward(t, n):
        pre = jnp.broadcast_to(bias[...], (n * HW, C))
        for a in range(3):
            for i in range(3):
                rows = xc[t + a : t + a + n, i : i + H].reshape(n * HW, K3)
                pre = pre + jnp.dot(rows, w[a * 3 + i], preferred_element_type=F32)
        sigma = jax.nn.sigmoid(pre)
        act[t : t + n] = (pre * sigma).astype(BF16).reshape(n, H, W, C)
        cot = og[t : t + n].reshape(n * HW, C).astype(F32)
        gate = (cot * sigma * (1.0 + pre * (1.0 - sigma))).astype(BF16)
        gc[t : t + n, 1 : H + 1, :, C : 2 * C] = gate.reshape(n, H, W, C)
        return jnp.sum(gate.astype(F32).reshape(n * HW // 8, 8, C), axis=0)

    bias_sum = jnp.zeros((8, C), F32)
    for t in range(2, F, 2):
        bias_sum = bias_sum + forward(t, 2)

    @pl.when(z > 0)
    def _():
        halo_copy().wait_recv()

    @pl.when(z == 0)
    def _():
        frames[0:2] = jnp.zeros((2, H, W, C), BF16)

    for e in range(2):
        spread(e)
    bias_sum = bias_sum + forward(0, 2)
    b_own[...] = bias_sum

    gate_out, gate_in = frames.at[pl.ds(F + 2, 2)], frames.at[pl.ds(F + 4, 2)]
    for t in range(2):
        frames[F + 2 + t] = gc[t, 1 : H + 1, :, C : 2 * C]

    @pl.when(z > 0)
    def _():
        gate_copy().start()

    half = Q * R

    def my_half(core):
        return pl.ds(pl.multiple_of(core * half, 16), half)

    def pair_copy(a):
        return remote(dwb.at[a, my_half(1 - c)], pair_in.at[a], p_s.at[a], p_r.at[a], other)

    def xy_copy(a, k):
        there = pl.ds(pl.multiple_of(((q + k) % Q) * R, 16), R)
        return remote(
            s16.at[a, there], xy_in.at[a, k], x_s.at[a, k], x_r.at[a, k], to_q(k)
        )

    def z_copy(k):
        there = pl.ds(pl.multiple_of(((z + k) % T) * U, 16), U)
        return remote(z16.at[there], z_in.at[k], zs_s.at[k], zs_r.at[k], to_z(k))

    def bias_pair():
        return remote(b_own, b_pair, bp_s, bp_r, other)

    def bias_q(k):
        return remote(bx.at[q], bx.at[q], bx_s.at[k], bx_r.at[k], to_q(k))

    def bias_z(k):
        return remote(bz.at[z], bz.at[z], bz_s.at[k], bz_r.at[k], to_z(k))

    def weight_term(a):
        gates = jnp.concatenate(
            [
                gc[0:F, 2 - i : 2 - i + H, :, C : 2 * C].reshape(F * HW, C)
                for i in range(3)
            ],
            axis=1,
        )
        term = jnp.dot(xt[:, a * HW : (a + F) * HW], gates, preferred_element_type=F32)
        for i in range(3):
            block = term[:, i * C : (i + 1) * C]
            dwf[a, i * K3 : (i + 1) * K3] = block
            dwb[a, i * K3 : (i + 1) * K3] = block.astype(BF16)

    def after_pair(a):
        pair_copy(a).wait_recv()
        both = dwf[a, my_half(c)] + pair_in[a].astype(F32)
        s32[a] = both
        s16[a] = both.astype(BF16)
        each(1, Q, lambda k: xy_copy(a, k).start())

    bias_pair().start()
    weight_term(0)
    pair_copy(0).start()
    weight_term(1)
    pair_copy(1).start()
    after_pair(0)
    weight_term(2)
    pair_copy(2).start()
    after_pair(1)
    bias_pair().wait_recv()
    bx[q] = b_own[...] + b_pair[...]
    each(1, Q, lambda k: bias_q(k).start())

    def spread_gate(t, mid):
        left, right = shifted(mid.astype(F32))
        gc[t, 1 : H + 1, :, 0:C] = right.reshape(H, W, C)
        gc[t, 1 : H + 1, :, 2 * C :] = left.reshape(H, W, C)

    for t in range(F):
        spread_gate(t, gc[t, 1 : H + 1, :, C : 2 * C].reshape(HW, C))
    after_pair(2)

    def backward(t, n):
        out = jnp.zeros((n * HW, C), F32)
        for a in range(3):
            for i in range(3):
                rows = gc[t + 2 - a : t + 2 - a + n, 2 - i : 2 - i + H].reshape(n * HW, K3)
                out = out + jnp.dot(rows, wt[a * 3 + i], preferred_element_type=F32)
        igrad[t : t + n] = out.astype(BF16).reshape(n, H, W, C)

    backward(0, 2)
    backward(2, 2)

    def after_xy(a):
        here = pl.ds(pl.multiple_of(q * R, 16), R)
        each(1, Q, lambda k: xy_copy(a, k).wait_recv())
        got = s32[a, here]
        for k in range(1, Q):
            got = got + xy_in[a, k].astype(F32)
        z32[a * R : (a + 1) * R] = got
        z16[a * R : (a + 1) * R] = got.astype(BF16)

    for a in range(3):
        after_xy(a)
    each(1, T, lambda k: z_copy(k).start())
    each(1, Q, lambda k: bias_q(k).wait_recv())
    got = bx[0]
    for k in range(1, Q):
        got = got + bx[k]
    bz[z] = got
    each(1, T, lambda k: bias_z(k).start())

    backward(4, 2)

    each(1, T, lambda k: z_copy(k).wait_recv())
    got = z32[pl.ds(pl.multiple_of(z * U, 16), U)]
    for k in range(1, T):
        got = got + z_in[k].astype(F32)
    block = c * Q + q
    total[block, z] = got.astype(BF16)

    def piece(k, kz):
        return total.at[c * Q + (q + Q - k) % Q, (z + T - kz) % T]

    def gather_z(k):
        return remote(piece(0, 0), piece(0, 0), az_s.at[k], az_r.at[k], to_z(k))

    def gather_q(kz, k):
        return remote(piece(0, kz), piece(0, kz), ax_s.at[kz, k], ax_r.at[kz, k], to_q(k))

    def gather_pair(kz, k):
        return remote(piece(k, kz), piece(k, kz), ap_s.at[kz, k], ap_r.at[kz, k], other)

    def send_on(kz):
        each(1, Q, lambda k: gather_q(kz, k).start())
        gather_pair(kz, 0).start()

    each(1, T, lambda k: gather_z(k).start())
    send_on(0)

    @pl.when(z < T - 1)
    def _():
        gate_copy().wait_recv()

    @pl.when(z == T - 1)
    def _():
        frames[F + 4 : F + 6] = jnp.zeros((2, H, W, C), BF16)

    for t in range(2):
        mid = frames[F + 4 + t]
        gc[F + t, 1 : H + 1, :, C : 2 * C] = mid
        spread_gate(F + t, mid.reshape(HW, C))

    def relay_z(kz):
        gather_z(kz).wait_recv()
        send_on(kz)

    def relay_q(kz):
        def one(k):
            gather_q(kz, k).wait_recv()
            gather_pair(kz, k).start()

        each(1, Q, one)

    each(1, T, relay_z)
    backward(6, 2)
    each(0, T, relay_q)

    each(1, T, lambda k: bias_z(k).wait_recv())
    got = bz[0]
    for k in range(1, T):
        got = got + bz[k]
    bgrad[...] = jnp.sum(got, axis=0, keepdims=True)

    each(0, T, lambda kz: each(0, Q, lambda k: gather_pair(kz, k).wait_recv()))

    each(1, T, lambda k: row_copy(k).wait_send())

    @pl.when(z < T - 1)
    def _():
        halo_copy().wait_send()

    @pl.when(z > 0)
    def _():
        gate_copy().wait_send()

    bias_pair().wait_send()
    each(1, Q, lambda k: bias_q(k).wait_send())
    each(1, T, lambda k: bias_z(k).wait_send())
    for a in range(3):
        pair_copy(a).wait_send()
        each(1, Q, lambda k: xy_copy(a, k).wait_send())
    each(1, T, lambda k: z_copy(k).wait_send())
    each(1, T, lambda k: gather_z(k).wait_send())
    each(0, T, lambda kz: each(1, Q, lambda k: gather_q(kz, k).wait_send()))
    each(0, T, lambda kz: each(0, Q, lambda k: gather_pair(kz, k).wait_send()))


def finish_body(
    D, R, scale, act, igrad, total, bgrad, act_out, igrad_out, kernel_out, bias_out,
    kernel_grad, bias_grad, sem,
):
    rows = kernel_grad.shape[1]
    copies = [
        pltpu.make_async_copy(act, act_out, sem.at[0]),
        pltpu.make_async_copy(igrad, igrad_out, sem.at[1]),
        pltpu.make_async_copy(bias_grad, bias_out, sem.at[2]),
    ]
    copies[0].start()
    copies[1].start()
    bias_grad[...] = bgrad[...] * scale
    copies[2].start()
    for a in range(3):
        for b in range(pl.cdiv(rows, R)):
            n = min(R, rows - b * R)
            kernel_grad[a, b * R : b * R + n] = total[b, a * R : a * R + n].astype(F32) * scale
        copies.append(pltpu.make_async_copy(kernel_grad.at[a], kernel_out.at[a], sem.at[3 + a]))
        copies[-1].start()
    for copy in copies:
        copy.wait()


def body(T, D, loaded, frame_index, out_grad, kernel, conv_bias):
    _, F, H, W, C = loaded.shape
    Q = D // 2
    K3, HW = 3 * C, H * W
    R = 16 * pl.cdiv(pl.cdiv(3 * K3, 16), D)
    U = 16 * pl.cdiv(3 * R // 16, T)
    dims = (T, D, F, H, W, C, R, U)
    vmem = pl.BlockSpec(memory_space=pltpu.VMEM)
    hbm = pl.BlockSpec(memory_space=pltpu.HBM)
    V = pltpu.VMEM
    S = pltpu.SemaphoreType.DMA
    act, igrad, total, bgrad = pl.pallas_call(
        functools.partial(kernel_body, dims),
        out_shape=(
            jax.ShapeDtypeStruct((F, H, W, C), BF16),
            jax.ShapeDtypeStruct((F, H, W, C), BF16),
            jax.ShapeDtypeStruct((D, T, U, C), BF16),
            jax.ShapeDtypeStruct((1, C), F32),
        ),
        in_specs=[hbm] * 5,
        out_specs=(vmem, vmem, vmem, vmem),
        scratch_shapes=[
            pltpu.SMEM((1, F), jnp.int32), V((F, H, W, C), BF16), V((1, C), F32),
            V((F, H, W, C), BF16), V((9, K3, C), BF16), V((9, K3, C), BF16),
            V((T, CAP * H + 1, W, C), BF16), V((T, CAP * H + 1, W, C), BF16),
            V((F + 6, H, W, C), BF16),
            V((F + 2, H + 2, W, K3), BF16), V((K3, (F + 2) * HW), BF16),
            V((F + 2, H + 2, W, K3), BF16),
            V((3, D * R, C), F32), V((3, D * R, C), BF16),
            V((3, Q * R, C), BF16), V((3, Q * R, C), F32), V((3, Q * R, C), BF16),
            V((3, Q, R, C), BF16), V((T * U, C), F32), V((T * U, C), BF16),
            V((T, U, C), BF16),
            V((8, C), F32), V((8, C), F32), V((Q, 8, C), F32), V((T, 8, C), F32),
            S((5,)), S((T,)), S((T,)), S, S, S, S,
            S((3,)), S((3,)), S((3, Q)), S((3, Q)), S((T,)), S((T,)),
            S((T,)), S((T,)), S((T, Q)), S((T, Q)), S((T, Q)), S((T, Q)),
            S, S, S((Q,)), S((Q,)), S((T,)), S((T,)),
        ],
        compiler_params=pltpu.CompilerParams(
            collective_id=0, has_side_effects=True, vmem_limit_bytes=48 * 1024 * 1024
        ),
    )(*(
        pltpu.with_memory_space_constraint(x, pltpu.HBM)
        for x in (frame_index, loaded[0], out_grad[0], kernel.reshape(9, K3, C), conv_bias[None])
    ))
    scale = 1.0 / math.sqrt(T * F * HW * D * loaded.shape[0])
    act, igrad, kernel_grad, bias_grad = pl.pallas_call(
        functools.partial(finish_body, D, R, scale),
        out_shape=(
            jax.ShapeDtypeStruct((F, H, W, C), BF16),
            jax.ShapeDtypeStruct((F, H, W, C), BF16),
            jax.ShapeDtypeStruct((3, 3 * K3, C), F32),
            jax.ShapeDtypeStruct((1, C), F32),
        ),
        in_specs=[vmem] * 4,
        out_specs=[hbm] * 4,
        scratch_shapes=[V((3, 3 * K3, C), F32), V((1, C), F32), S((6,))],
        compiler_params=pltpu.CompilerParams(vmem_limit_bytes=8 * 1024 * 1024),
    )(act, igrad, total.reshape(D, T * U, C), bgrad)
    return act[None], igrad[None], kernel_grad.reshape(kernel.shape), bias_grad[0]


def solution(mesh):
    spread = P("dp", "tm", None, None, None)
    return jax.shard_map(
        functools.partial(body, mesh.shape["tm"], mesh.shape["dp"]),
        mesh=mesh,
        in_specs=(spread, P("dp", "tm"), spread, P(), P()),
        out_specs=(spread, spread, P(), P()),
        check_vma=False,
    )
```

```python
import functools
import math

import jax
import jax.numpy as jnp
from jax import lax
from jax.experimental import pallas as pl
from jax.experimental.pallas import tpu as pltpu
from jax.sharding import PartitionSpec as P

CAP = 3
F32, BF16 = jnp.float32, jnp.bfloat16


def each(first, last, step):
    if last - first <= 4:
        for i in range(first, last):
            step(i)
    else:
        lax.fori_loop(first, last, lambda i, carry: (step(i), carry)[1], 0)


def kernel_body(
    dims, ids_hbm, loaded_hbm, og_hbm, w_hbm, bias_hbm,
    act, igrad, total, bgrad,
    ids, loaded, bias, og, w, wt, slots, rslots, frames, xc, xt, gc, dwf, dwb,
    pair_in, s32, s16, xy_in, z32, z16, z_in, b_own, b_pair, bx, bz,
    ld_sem, f_s, f_r, h_s, h_r, g_s, g_r, p_s, p_r, x_s, x_r, zs_s, zs_r,
    az_s, az_r, ax_s, ax_r, ap_s, ap_r, bp_s, bp_r, bx_s, bx_r, bz_s, bz_r,
):
    T, D, F, H, W, C, R, U, pieces = dims
    Q = D // 2
    HW = H * W
    K3 = 3 * C
    z = lax.axis_index("tm")
    dp = lax.axis_index("dp")
    c, q = dp % 2, dp // 2

    def at(tm=None, chip=None, core=None):
        return {
            "tm": z if tm is None else tm,
            "dp": (q if chip is None else chip) * 2 + (c if core is None else core),
        }

    def to_z(k):
        return at(tm=(z + k) % T)

    def to_q(k):
        return at(chip=(q + k) % Q)

    other = at(core=1 - c)

    def remote(src, dst, ss, rs, where):
        return pltpu.make_async_remote_copy(
            src_ref=src, dst_ref=dst, send_sem=ss, recv_sem=rs,
            device_id=where, device_id_type=pl.DeviceIdType.MESH,
        )

    loads = [
        pltpu.make_async_copy(source, target, ld_sem.at[n])
        for n, (source, target) in enumerate(
            [(ids_hbm, ids), (loaded_hbm, loaded), (w_hbm, w), (og_hbm, og), (bias_hbm, bias)]
        )
    ]
    for load in loads:
        load.start()

    barrier = pltpu.get_barrier_semaphore()

    def greet(where):
        pl.semaphore_signal(barrier, 1, device_id=where, device_id_type=pl.DeviceIdType.MESH)

    greet(other)
    each(1, Q, lambda k: greet(to_q(k)))
    each(1, T, lambda k: greet(to_z(k)))

    loads[0].wait()
    loads[1].wait()

    owners = [ids[0, r] // F for r in range(F)]
    rank = []
    for r in range(F):
        before = jnp.int32(0)
        for s in range(r):
            before = before + jnp.where(owners[s] == owners[r], 1, 0)
        rank.append(before)

    line = lax.broadcasted_iota(jnp.int32, (W, C), 0)

    def pack(k):
        owner = (z + k) % T
        targets = jnp.zeros((W, C), F32)
        for s in range(CAP):
            row, target = jnp.int32(0), jnp.int32(-1)
            for r in range(F):
                hit = jnp.logical_and(owners[r] == owner, rank[r] == s)
                row = jnp.where(hit, r, row)
                target = jnp.where(hit, ids[0, r] - owner * F, target)
            slots[k, s * H : (s + 1) * H] = loaded[row]
            targets = jnp.where(line == s, target.astype(F32), targets)
        slots[k, CAP * H] = targets.astype(BF16)

    each(0, T, pack)
    pl.semaphore_wait(barrier, 1 + (Q - 1) + (T - 1))

    def row_copy(k):
        return remote(slots.at[k], rslots.at[k], f_s.at[k], f_r.at[k], to_z(k))

    each(1, T, lambda k: row_copy(k).start())

    for e in range(F + 2):
        for ref in (xc, gc):
            ref[e, 0] = jnp.zeros((W, K3), BF16)
            ref[e, H + 1] = jnp.zeros((W, K3), BF16)
    taps_rows = 3 * K3
    if D * R > taps_rows:
        for a in range(3):
            dwf[a, taps_rows:] = jnp.zeros((D * R - taps_rows, C), F32)
            dwb[a, taps_rows:] = jnp.zeros((D * R - taps_rows, C), BF16)
    if pieces * U > R:
        for a in range(3):
            z32[a, R:] = jnp.zeros((pieces * U - R, C), F32)
            z16[a, R:] = jnp.zeros((pieces * U - R, C), BF16)
    loads[2].wait()
    for p in range(9):
        for j in range(3):
            wt[p, j * C : (j + 1) * C, :] = w[p, j * C : (j + 1) * C, :].T
    loads[3].wait()
    loads[4].wait()

    each(1, T, lambda k: row_copy(k).wait_recv())

    def place(f):
        picked = jnp.zeros((H, W, C), BF16)
        for k in range(T):
            source = slots if k == 0 else rslots
            for s in range(CAP):
                gap = jnp.abs(source[k, CAP * H, s : s + 1].astype(F32) - f)
                weight = jnp.broadcast_to(jnp.maximum(1.0 - gap, 0.0), (W, C)).astype(BF16)
                picked = picked + source[k, s * H : (s + 1) * H] * weight[None]
        frames[f + 2] = picked

    for f in (F - 2, F - 1):
        place(f)

    def halo_copy():
        return remote(frames.at[pl.ds(F, 2)], frames.at[pl.ds(0, 2)], h_s, h_r, to_z(1))

    def gate_copy():
        return remote(
            gate_out, gate_in, g_s, g_r, to_z(T - 1)
        )

    @pl.when(z < T - 1)
    def _():
        halo_copy().start()

    for f in range(F - 2):
        place(f)

    column = lax.broadcasted_iota(jnp.int32, (HW, C), 0) % W

    def shifted(value):
        left = jnp.where(column == 0, 0.0, pltpu.roll(value, 1, 0))
        right = jnp.where(column == W - 1, 0.0, pltpu.roll(value, HW - 1, 0))
        return left.astype(BF16), right.astype(BF16)

    def spread(e):
        mid = frames[e].reshape(HW, C)
        left, right = shifted(mid.astype(F32))
        for j, part in enumerate((left, mid, right)):
            xc[e, 1 : H + 1, :, j * C : (j + 1) * C] = part.reshape(H, W, C)
            xt[j * C : (j + 1) * C, e * HW : (e + 1) * HW] = part.T

    for e in range(2, F + 2):
        spread(e)

    def forward(t, n):
        pre = jnp.broadcast_to(bias[...], (n * HW, C))
        for a in range(3):
            for i in range(3):
                rows = xc[t + a : t + a + n, i : i + H].reshape(n * HW, K3)
                pre = pre + jnp.dot(rows, w[a * 3 + i], preferred_element_type=F32)
        sigma = jax.nn.sigmoid(pre)
        act[t : t + n] = (pre * sigma).astype(BF16).reshape(n, H, W, C)
        cot = og[t : t + n].reshape(n * HW, C).astype(F32)
        gate = (cot * sigma * (1.0 + pre * (1.0 - sigma))).astype(BF16)
        gc[t : t + n, 1 : H + 1, :, C : 2 * C] = gate.reshape(n, H, W, C)
        return jnp.sum(gate.astype(F32).reshape(n * HW // 8, 8, C), axis=0)

    bias_sum = jnp.zeros((8, C), F32)
    for t in range(2, F, 2):
        bias_sum = bias_sum + forward(t, 2)

    @pl.when(z > 0)
    def _():
        halo_copy().wait_recv()

    @pl.when(z == 0)
    def _():
        frames[0:2] = jnp.zeros((2, H, W, C), BF16)

    for e in range(2):
        spread(e)
    bias_sum = bias_sum + forward(0, 2)
    b_own[...] = bias_sum

    gate_out, gate_in = frames.at[pl.ds(F + 2, 2)], frames.at[pl.ds(F + 4, 2)]
    for t in range(2):
        frames[F + 2 + t] = gc[t, 1 : H + 1, :, C : 2 * C]

    @pl.when(z > 0)
    def _():
        gate_copy().start()

    half = Q * R

    def my_half(core):
        return pl.ds(pl.multiple_of(core * half, 16), half)

    def pair_copy(a):
        return remote(dwb.at[a, my_half(1 - c)], pair_in.at[a], p_s.at[a], p_r.at[a], other)

    def xy_copy(a, k):
        there = pl.ds(pl.multiple_of(((q + k) % Q) * R, 16), R)
        return remote(
            s16.at[a, there], xy_in.at[a, k], x_s.at[a, k], x_r.at[a, k], to_q(k)
        )

    def duty(a, k):
        return (z + k + 4 * T - a) % T

    def if_duty(a, k, action):
        pl.when(duty(a, k) < pieces)(action)

    def piece_rows(a, k):
        return pl.ds(pl.multiple_of(jnp.minimum(duty(a, k), pieces - 1) * U, 16), U)

    def z_copy(a, k):
        there = piece_rows(a, k)
        return remote(z16.at[a, there], z_in.at[a, k], zs_s.at[a, k], zs_r.at[a, k], to_z(k))

    def bias_pair():
        return remote(b_own, b_pair, bp_s, bp_r, other)

    def bias_q(k):
        return remote(bx.at[q], bx.at[q], bx_s.at[k], bx_r.at[k], to_q(k))

    def bias_z(k):
        return remote(bz.at[z], bz.at[z], bz_s.at[k], bz_r.at[k], to_z(k))

    def weight_term(a):
        gates = jnp.concatenate(
            [
                gc[0:F, 2 - i : 2 - i + H, :, C : 2 * C].reshape(F * HW, C)
                for i in range(3)
            ],
            axis=1,
        )
        term = jnp.dot(xt[:, a * HW : (a + F) * HW], gates, preferred_element_type=F32)
        for i in range(3):
            block = term[:, i * C : (i + 1) * C]
            dwf[a, i * K3 : (i + 1) * K3] = block
            dwb[a, i * K3 : (i + 1) * K3] = block.astype(BF16)

    def after_pair(a):
        pair_copy(a).wait_recv()
        both = dwf[a, my_half(c)] + pair_in[a].astype(F32)
        s32[a] = both
        s16[a] = both.astype(BF16)
        each(1, Q, lambda k: xy_copy(a, k).start())

    bias_pair().start()
    weight_term(0)
    pair_copy(0).start()
    weight_term(1)
    pair_copy(1).start()
    after_pair(0)
    weight_term(2)
    pair_copy(2).start()
    after_pair(1)
    bias_pair().wait_recv()
    bx[q] = b_own[...] + b_pair[...]
    each(1, Q, lambda k: bias_q(k).start())

    def spread_gate(t, mid):
        left, right = shifted(mid.astype(F32))
        gc[t, 1 : H + 1, :, 0:C] = right.reshape(H, W, C)
        gc[t, 1 : H + 1, :, 2 * C :] = left.reshape(H, W, C)

    for t in range(F):
        spread_gate(t, gc[t, 1 : H + 1, :, C : 2 * C].reshape(HW, C))
    after_pair(2)

    def backward(t, n):
        out = jnp.zeros((n * HW, C), F32)
        for a in range(3):
            for i in range(3):
                rows = gc[t + 2 - a : t + 2 - a + n, 2 - i : 2 - i + H].reshape(n * HW, K3)
                out = out + jnp.dot(rows, wt[a * 3 + i], preferred_element_type=F32)
        igrad[t : t + n] = out.astype(BF16).reshape(n, H, W, C)

    def after_xy(a):
        here = pl.ds(pl.multiple_of(q * R, 16), R)
        each(1, Q, lambda k: xy_copy(a, k).wait_recv())
        got = s32[a, here]
        for k in range(1, Q):
            got = got + xy_in[a, k].astype(F32)
        z32[a, 0:R] = got
        z16[a, 0:R] = got.astype(BF16)
        each(1, T, lambda k: if_duty(a, k, lambda: z_copy(a, k).start()))

    def gather_z(a, k):
        piece = total.at[c * Q + q, a, piece_rows(a, 0)]
        return remote(piece, piece, az_s.at[a, k], az_r.at[a, k], to_z(k))

    def gather_q(a, kz, k):
        piece = total.at[c * Q + q, a, piece_rows(a, -kz)]
        return remote(piece, piece, ax_s.at[a, kz, k], ax_r.at[a, kz, k], to_q(k))

    def gather_pair(a, k):
        block = total.at[c * Q + (q + Q - k) % Q, a]
        return remote(block, block, ap_s.at[a, k], ap_r.at[a, k], other)

    def after_z(a):
        def sum_up():
            each(1, T, lambda k: z_copy(a, k).wait_recv())
            got = z32[a, piece_rows(a, 0)]
            for k in range(1, T):
                got = got + z_in[a, k].astype(F32)
            total[c * Q + q, a, piece_rows(a, 0)] = got.astype(BF16)
            each(1, T, lambda k: gather_z(a, k).start())
            each(1, Q, lambda k: gather_q(a, 0, k).start())

        if_duty(a, 0, sum_up)

    def relay_z(a):
        def one(kz):
            def pass_on():
                gather_z(a, kz).wait_recv()
                each(1, Q, lambda k: gather_q(a, kz, k).start())

            if_duty(a, -kz, pass_on)

        each(1, T, one)
        gather_pair(a, 0).start()

    def relay_q(a):
        def one(k):
            each(0, T, lambda kz: if_duty(a, -kz, lambda: gather_q(a, kz, k).wait_recv()))
            gather_pair(a, k).start()

        each(1, Q, one)

    backward(0, 2)
    after_xy(0)
    backward(2, 2)
    after_xy(1)
    after_xy(2)
    each(1, Q, lambda k: bias_q(k).wait_recv())
    got = bx[0]
    for k in range(1, Q):
        got = got + bx[k]
    bz[z] = got
    each(1, T, lambda k: bias_z(k).start())
    backward(4, 2)
    after_z(0)
    after_z(1)

    @pl.when(z < T - 1)
    def _():
        gate_copy().wait_recv()

    @pl.when(z == T - 1)
    def _():
        frames[F + 4 : F + 6] = jnp.zeros((2, H, W, C), BF16)

    for t in range(2):
        mid = frames[F + 4 + t]
        gc[F + t, 1 : H + 1, :, C : 2 * C] = mid
        spread_gate(F + t, mid.reshape(HW, C))
    after_z(2)
    relay_z(0)
    backward(6, 2)
    relay_z(1)
    relay_q(0)
    relay_z(2)
    relay_q(1)
    relay_q(2)

    each(1, T, lambda k: bias_z(k).wait_recv())
    got = bz[0]
    for k in range(1, T):
        got = got + bz[k]
    bgrad[...] = jnp.sum(got, axis=0, keepdims=True)

    each(0, 3, lambda a: each(0, Q, lambda k: gather_pair(a, k).wait_recv()))

    each(1, T, lambda k: row_copy(k).wait_send())

    @pl.when(z < T - 1)
    def _():
        halo_copy().wait_send()

    @pl.when(z > 0)
    def _():
        gate_copy().wait_send()

    bias_pair().wait_send()
    each(1, Q, lambda k: bias_q(k).wait_send())
    each(1, T, lambda k: bias_z(k).wait_send())
    for a in range(3):
        pair_copy(a).wait_send()
        each(1, Q, lambda k: xy_copy(a, k).wait_send())
    for a in range(3):
        each(1, T, lambda k: if_duty(a, k, lambda: z_copy(a, k).wait_send()))

        def gathered():
            each(1, T, lambda k: gather_z(a, k).wait_send())

        if_duty(a, 0, gathered)

        def passed_on(kz):
            def sent():
                each(1, Q, lambda k: gather_q(a, kz, k).wait_send())

            if_duty(a, -kz, sent)

        each(0, T, passed_on)
        each(0, Q, lambda k: gather_pair(a, k).wait_send())


def finish_body(
    D, R, scale, act, igrad, total, bgrad, act_out, igrad_out, kernel_out, bias_out,
    kernel_grad, bias_grad, sem,
):
    rows = kernel_grad.shape[1]
    copies = [
        pltpu.make_async_copy(act, act_out, sem.at[0]),
        pltpu.make_async_copy(igrad, igrad_out, sem.at[1]),
        pltpu.make_async_copy(bias_grad, bias_out, sem.at[2]),
    ]
    copies[0].start()
    copies[1].start()
    bias_grad[...] = bgrad[...] * scale
    copies[2].start()
    for a in range(3):
        for b in range(pl.cdiv(rows, R)):
            n = min(R, rows - b * R)
            kernel_grad[a, b * R : b * R + n] = total[b, a, 0:n].astype(F32) * scale
        copies.append(pltpu.make_async_copy(kernel_grad.at[a], kernel_out.at[a], sem.at[3 + a]))
        copies[-1].start()
    for copy in copies:
        copy.wait()


def body(T, D, loaded, frame_index, out_grad, kernel, conv_bias):
    _, F, H, W, C = loaded.shape
    Q = D // 2
    K3, HW = 3 * C, H * W
    R = 16 * pl.cdiv(pl.cdiv(3 * K3, 16), D)
    U = 16 * pl.cdiv(R // 16, T)
    pieces = pl.cdiv(R, U)
    dims = (T, D, F, H, W, C, R, U, pieces)
    vmem = pl.BlockSpec(memory_space=pltpu.VMEM)
    hbm = pl.BlockSpec(memory_space=pltpu.HBM)
    V = pltpu.VMEM
    S = pltpu.SemaphoreType.DMA
    act, igrad, total, bgrad = pl.pallas_call(
        functools.partial(kernel_body, dims),
        out_shape=(
            jax.ShapeDtypeStruct((F, H, W, C), BF16),
            jax.ShapeDtypeStruct((F, H, W, C), BF16),
            jax.ShapeDtypeStruct((D, 3, pieces * U, C), BF16),
            jax.ShapeDtypeStruct((1, C), F32),
        ),
        in_specs=[hbm] * 5,
        out_specs=(vmem, vmem, vmem, vmem),
        scratch_shapes=[
            pltpu.SMEM((1, F), jnp.int32), V((F, H, W, C), BF16), V((1, C), F32),
            V((F, H, W, C), BF16), V((9, K3, C), BF16), V((9, K3, C), BF16),
            V((T, CAP * H + 1, W, C), BF16), V((T, CAP * H + 1, W, C), BF16),
            V((F + 6, H, W, C), BF16),
            V((F + 2, H + 2, W, K3), BF16), V((K3, (F + 2) * HW), BF16),
            V((F + 2, H + 2, W, K3), BF16),
            V((3, D * R, C), F32), V((3, D * R, C), BF16),
            V((3, Q * R, C), BF16), V((3, Q * R, C), F32), V((3, Q * R, C), BF16),
            V((3, Q, R, C), BF16), V((3, pieces * U, C), F32), V((3, pieces * U, C), BF16),
            V((3, T, U, C), BF16),
            V((8, C), F32), V((8, C), F32), V((Q, 8, C), F32), V((T, 8, C), F32),
            S((5,)), S((T,)), S((T,)), S, S, S, S,
            S((3,)), S((3,)), S((3, Q)), S((3, Q)), S((3, T)), S((3, T)),
            S((3, T)), S((3, T)), S((3, T, Q)), S((3, T, Q)), S((3, Q)), S((3, Q)),
            S, S, S((Q,)), S((Q,)), S((T,)), S((T,)),
        ],
        compiler_params=pltpu.CompilerParams(
            collective_id=0, has_side_effects=True, vmem_limit_bytes=48 * 1024 * 1024
        ),
    )(*(
        pltpu.with_memory_space_constraint(x, pltpu.HBM)
        for x in (frame_index, loaded[0], out_grad[0], kernel.reshape(9, K3, C), conv_bias[None])
    ))
    scale = 1.0 / math.sqrt(T * F * HW * D * loaded.shape[0])
    act, igrad, kernel_grad, bias_grad = pl.pallas_call(
        functools.partial(finish_body, D, R, scale),
        out_shape=(
            jax.ShapeDtypeStruct((F, H, W, C), BF16),
            jax.ShapeDtypeStruct((F, H, W, C), BF16),
            jax.ShapeDtypeStruct((3, 3 * K3, C), F32),
            jax.ShapeDtypeStruct((1, C), F32),
        ),
        in_specs=[vmem] * 4,
        out_specs=[hbm] * 4,
        scratch_shapes=[V((3, 3 * K3, C), F32), V((1, C), F32), S((6,))],
        compiler_params=pltpu.CompilerParams(vmem_limit_bytes=8 * 1024 * 1024),
    )(act, igrad, total, bgrad)
    return act[None], igrad[None], kernel_grad.reshape(kernel.shape), bias_grad[0]


def solution(mesh):
    spread = P("dp", "tm", None, None, None)
    return jax.shard_map(
        functools.partial(body, mesh.shape["tm"], mesh.shape["dp"]),
        mesh=mesh,
        in_specs=(spread, P("dp", "tm"), spread, P(), P()),
        out_specs=(spread, spread, P(), P()),
        check_vma=False,
    )
```

```python
import functools
import math

import jax
import jax.numpy as jnp
from jax import lax
from jax.experimental import pallas as pl
from jax.experimental.pallas import tpu as pltpu
from jax.sharding import PartitionSpec as P

CAP = 3
F32, BF16 = jnp.float32, jnp.bfloat16


def each(first, last, step):
    if last - first <= 4:
        for i in range(first, last):
            step(i)
    else:
        lax.fori_loop(first, last, lambda i, carry: (step(i), carry)[1], 0)


def kernel_body(
    dims, ids_hbm, loaded_hbm, og_hbm, w_hbm, bias_hbm,
    act, igrad, total, bgrad,
    ids, loaded, bias, og, w, wt, slots, rslots, frames, xc, xt, gc, dwf, dwb,
    pair_in, s32, s16, xy_in, z32, z16, z_in, b_own, b_pair, bx, bz,
    ld_sem, f_s, f_r, h_s, h_r, g_s, g_r, p_s, p_r, x_s, x_r, zs_s, zs_r,
    az_s, az_r, ax_s, ax_r, ap_s, ap_r, bp_s, bp_r, bx_s, bx_r, bz_s, bz_r,
):
    T, D, F, H, W, C, R, U, pieces = dims
    Q = D // 2
    HW = H * W
    K3 = 3 * C
    z = lax.axis_index("tm")
    dp = lax.axis_index("dp")
    c, q = dp % 2, dp // 2

    def at(tm=None, chip=None, core=None):
        return {
            "tm": z if tm is None else tm,
            "dp": (q if chip is None else chip) * 2 + (c if core is None else core),
        }

    def to_z(k):
        return at(tm=(z + k) % T)

    def to_q(k):
        return at(chip=(q + k) % Q)

    other = at(core=1 - c)

    def remote(src, dst, ss, rs, where):
        return pltpu.make_async_remote_copy(
            src_ref=src, dst_ref=dst, send_sem=ss, recv_sem=rs,
            device_id=where, device_id_type=pl.DeviceIdType.MESH,
        )

    loads = [
        pltpu.make_async_copy(source, target, ld_sem.at[n])
        for n, (source, target) in enumerate(
            [(ids_hbm, ids), (loaded_hbm, loaded), (w_hbm, w), (og_hbm, og), (bias_hbm, bias)]
        )
    ]
    for load in loads:
        load.start()

    barrier = pltpu.get_barrier_semaphore()

    def greet(where):
        pl.semaphore_signal(barrier, 1, device_id=where, device_id_type=pl.DeviceIdType.MESH)

    greet(other)
    each(1, Q, lambda k: greet(to_q(k)))
    each(1, T, lambda k: greet(to_z(k)))

    loads[0].wait()
    loads[1].wait()

    owners = [ids[0, r] // F for r in range(F)]
    rank = []
    for r in range(F):
        before = jnp.int32(0)
        for s in range(r):
            before = before + jnp.where(owners[s] == owners[r], 1, 0)
        rank.append(before)

    line = lax.broadcasted_iota(jnp.int32, (W, C), 0)

    def pack(k):
        owner = (z + k) % T
        targets = jnp.zeros((W, C), F32)
        for s in range(CAP):
            row, target = jnp.int32(0), jnp.int32(-1)
            for r in range(F):
                hit = jnp.logical_and(owners[r] == owner, rank[r] == s)
                row = jnp.where(hit, r, row)
                target = jnp.where(hit, ids[0, r] - owner * F, target)
            slots[k, s * H : (s + 1) * H] = loaded[row]
            targets = jnp.where(line == s, target.astype(F32), targets)
        slots[k, CAP * H] = targets.astype(BF16)

    each(0, T, pack)
    pl.semaphore_wait(barrier, 1 + (Q - 1) + (T - 1))

    def row_copy(k):
        return remote(slots.at[k], rslots.at[k], f_s.at[k], f_r.at[k], to_z(k))

    each(1, T, lambda k: row_copy(k).start())

    for e in range(F + 2):
        for ref in (xc, gc):
            ref[e, 0] = jnp.zeros((W, K3), BF16)
            ref[e, H + 1] = jnp.zeros((W, K3), BF16)
    taps_rows = 3 * K3
    if D * R > taps_rows:
        for a in range(3):
            dwf[a, taps_rows:] = jnp.zeros((D * R - taps_rows, C), F32)
            dwb[a, taps_rows:] = jnp.zeros((D * R - taps_rows, C), BF16)
    if pieces * U > R:
        for a in range(3):
            z32[a, R:] = jnp.zeros((pieces * U - R, C), F32)
            z16[a, R:] = jnp.zeros((pieces * U - R, C), BF16)
    loads[2].wait()
    for p in range(9):
        for j in range(3):
            wt[p, j * C : (j + 1) * C, :] = w[p, j * C : (j + 1) * C, :].T
    loads[3].wait()
    loads[4].wait()

    each(1, T, lambda k: row_copy(k).wait_recv())

    def place(f):
        picked = jnp.zeros((H, W, C), BF16)
        for k in range(T):
            source = slots if k == 0 else rslots
            for s in range(CAP):
                gap = jnp.abs(source[k, CAP * H, s : s + 1].astype(F32) - f)
                weight = jnp.broadcast_to(jnp.maximum(1.0 - gap, 0.0), (W, C)).astype(BF16)
                picked = picked + source[k, s * H : (s + 1) * H] * weight[None]
        frames[f + 2] = picked

    for f in (F - 2, F - 1):
        place(f)

    def halo_copy():
        return remote(frames.at[pl.ds(F, 2)], frames.at[pl.ds(0, 2)], h_s, h_r, to_z(1))

    def gate_copy():
        return remote(
            gate_out, gate_in, g_s, g_r, to_z(T - 1)
        )

    @pl.when(z < T - 1)
    def _():
        halo_copy().start()

    for f in range(F - 2):
        place(f)

    column = lax.broadcasted_iota(jnp.int32, (HW, C), 0) % W

    def shifted(value):
        left = jnp.where(column == 0, 0.0, pltpu.roll(value, 1, 0))
        right = jnp.where(column == W - 1, 0.0, pltpu.roll(value, HW - 1, 0))
        return left.astype(BF16), right.astype(BF16)

    def spread(e):
        mid = frames[e].reshape(HW, C)
        left, right = shifted(mid.astype(F32))
        for j, part in enumerate((left, mid, right)):
            xc[e, 1 : H + 1, :, j * C : (j + 1) * C] = part.reshape(H, W, C)
            xt[j * C : (j + 1) * C, e * HW : (e + 1) * HW] = part.T

    for e in range(2, F + 2):
        spread(e)

    def forward(t, n):
        pre = jnp.broadcast_to(bias[...], (n * HW, C))
        for a in range(3):
            for i in range(3):
                rows = xc[t + a : t + a + n, i : i + H].reshape(n * HW, K3)
                pre = pre + jnp.dot(rows, w[a * 3 + i], preferred_element_type=F32)
        sigma = jax.nn.sigmoid(pre)
        act[t : t + n] = (pre * sigma).astype(BF16).reshape(n, H, W, C)
        cot = og[t : t + n].reshape(n * HW, C).astype(F32)
        gate = (cot * sigma * (1.0 + pre * (1.0 - sigma))).astype(BF16)
        gc[t : t + n, 1 : H + 1, :, C : 2 * C] = gate.reshape(n, H, W, C)
        return jnp.sum(gate.astype(F32).reshape(n * HW // 8, 8, C), axis=0)

    bias_sum = jnp.zeros((8, C), F32)
    for t in range(2, F, 2):
        bias_sum = bias_sum + forward(t, 2)

    @pl.when(z > 0)
    def _():
        halo_copy().wait_recv()

    @pl.when(z == 0)
    def _():
        frames[0:2] = jnp.zeros((2, H, W, C), BF16)

    for e in range(2):
        spread(e)
    bias_sum = bias_sum + forward(0, 2)
    b_own[...] = bias_sum

    gate_out, gate_in = frames.at[pl.ds(F + 2, 2)], frames.at[pl.ds(F + 4, 2)]
    for t in range(2):
        frames[F + 2 + t] = gc[t, 1 : H + 1, :, C : 2 * C]

    @pl.when(z > 0)
    def _():
        gate_copy().start()

    half = Q * R

    def my_half(core):
        return pl.ds(pl.multiple_of(core * half, 16), half)

    def pair_copy(a):
        return remote(dwb.at[a, my_half(1 - c)], pair_in.at[a], p_s.at[a], p_r.at[a], other)

    def xy_copy(a, k):
        there = pl.ds(pl.multiple_of(((q + k) % Q) * R, 16), R)
        return remote(
            s16.at[a, there], xy_in.at[a, k], x_s.at[a, k], x_r.at[a, k], to_q(k)
        )

    def duty(a, k):
        return (z + k + 4 * T - a) % T

    def if_duty(a, k, action):
        pl.when(duty(a, k) < pieces)(action)

    def piece_rows(a, k):
        return pl.ds(pl.multiple_of(jnp.minimum(duty(a, k), pieces - 1) * U, 16), U)

    def z_copy(a, k):
        there = piece_rows(a, k)
        return remote(z16.at[a, there], z_in.at[a, k], zs_s.at[a, k], zs_r.at[a, k], to_z(k))

    def bias_pair():
        return remote(b_own, b_pair, bp_s, bp_r, other)

    def bias_q(k):
        return remote(bx.at[q], bx.at[q], bx_s.at[k], bx_r.at[k], to_q(k))

    def bias_z(k):
        return remote(bz.at[z], bz.at[z], bz_s.at[k], bz_r.at[k], to_z(k))

    def weight_term(a):
        gates = jnp.concatenate(
            [
                gc[0:F, 2 - i : 2 - i + H, :, C : 2 * C].reshape(F * HW, C)
                for i in range(3)
            ],
            axis=1,
        )
        term = jnp.dot(xt[:, a * HW : (a + F) * HW], gates, preferred_element_type=F32)
        for i in range(3):
            block = term[:, i * C : (i + 1) * C]
            dwf[a, i * K3 : (i + 1) * K3] = block
            dwb[a, i * K3 : (i + 1) * K3] = block.astype(BF16)

    def after_pair(a):
        pair_copy(a).wait_recv()
        both = dwf[a, my_half(c)] + pair_in[a].astype(F32)
        s32[a] = both
        s16[a] = both.astype(BF16)
        each(1, Q, lambda k: xy_copy(a, k).start())

    bias_pair().start()
    weight_term(0)
    pair_copy(0).start()
    weight_term(1)
    pair_copy(1).start()
    after_pair(0)
    weight_term(2)
    pair_copy(2).start()
    after_pair(1)
    bias_pair().wait_recv()
    bx[q] = b_own[...] + b_pair[...]
    each(1, Q, lambda k: bias_q(k).start())

    def spread_gate(t, mid):
        left, right = shifted(mid.astype(F32))
        gc[t, 1 : H + 1, :, 0:C] = right.reshape(H, W, C)
        gc[t, 1 : H + 1, :, 2 * C :] = left.reshape(H, W, C)

    for t in range(F):
        spread_gate(t, gc[t, 1 : H + 1, :, C : 2 * C].reshape(HW, C))
    after_pair(2)

    def backward(t, n):
        out = jnp.zeros((n * HW, C), F32)
        for a in range(3):
            for i in range(3):
                rows = gc[t + 2 - a : t + 2 - a + n, 2 - i : 2 - i + H].reshape(n * HW, K3)
                out = out + jnp.dot(rows, wt[a * 3 + i], preferred_element_type=F32)
        igrad[t : t + n] = out.astype(BF16).reshape(n, H, W, C)

    def after_xy(a):
        here = pl.ds(pl.multiple_of(q * R, 16), R)
        each(1, Q, lambda k: xy_copy(a, k).wait_recv())
        got = s32[a, here]
        for k in range(1, Q):
            got = got + xy_in[a, k].astype(F32)
        z32[a, 0:R] = got
        z16[a, 0:R] = got.astype(BF16)
        each(1, T, lambda k: if_duty(a, k, lambda: z_copy(a, k).start()))

    def gather_z(a, k):
        piece = total.at[c * Q + q, a, piece_rows(a, 0)]
        return remote(piece, piece, az_s.at[a, k], az_r.at[a, k], to_z(k))

    def gather_q(a, kz, k):
        piece = total.at[c * Q + q, a, piece_rows(a, -kz)]
        return remote(piece, piece, ax_s.at[a, kz, k], ax_r.at[a, kz, k], to_q(k))

    def gather_pair(a, k):
        block = total.at[c * Q + (q + Q - k) % Q, a]
        return remote(block, block, ap_s.at[a, k], ap_r.at[a, k], other)

    def after_z(a):
        def sum_up():
            each(1, T, lambda k: z_copy(a, k).wait_recv())
            got = z32[a, piece_rows(a, 0)]
            for k in range(1, T):
                got = got + z_in[a, k].astype(F32)
            total[c * Q + q, a, piece_rows(a, 0)] = got.astype(BF16)
            each(1, T, lambda k: gather_z(a, k).start())
            each(1, Q, lambda k: gather_q(a, 0, k).start())

        if_duty(a, 0, sum_up)

    def relay_z(a):
        def one(kz):
            def pass_on():
                gather_z(a, kz).wait_recv()
                each(1, Q, lambda k: gather_q(a, kz, k).start())

            if_duty(a, -kz, pass_on)

        each(1, T, one)
        gather_pair(a, 0).start()

    def relay_q(a):
        def one(k):
            each(0, T, lambda kz: if_duty(a, -kz, lambda: gather_q(a, kz, k).wait_recv()))
            gather_pair(a, k).start()

        each(1, Q, one)

    backward(0, 2)
    after_xy(0)
    backward(2, 2)
    after_xy(1)
    backward(4, 2)
    after_z(0)
    after_xy(2)

    @pl.when(z < T - 1)
    def _():
        gate_copy().wait_recv()

    @pl.when(z == T - 1)
    def _():
        frames[F + 4 : F + 6] = jnp.zeros((2, H, W, C), BF16)

    for t in range(2):
        mid = frames[F + 4 + t]
        gc[F + t, 1 : H + 1, :, C : 2 * C] = mid
        spread_gate(F + t, mid.reshape(HW, C))
    relay_z(0)
    after_z(1)
    each(1, Q, lambda k: bias_q(k).wait_recv())
    got = bx[0]
    for k in range(1, Q):
        got = got + bx[k]
    bz[z] = got
    each(1, T, lambda k: bias_z(k).start())
    backward(6, 2)
    relay_q(0)
    relay_z(1)
    after_z(2)
    relay_q(1)
    relay_z(2)
    relay_q(2)

    each(1, T, lambda k: bias_z(k).wait_recv())
    got = bz[0]
    for k in range(1, T):
        got = got + bz[k]
    bgrad[...] = jnp.sum(got, axis=0, keepdims=True)

    each(0, 3, lambda a: each(0, Q, lambda k: gather_pair(a, k).wait_recv()))

    each(1, T, lambda k: row_copy(k).wait_send())

    @pl.when(z < T - 1)
    def _():
        halo_copy().wait_send()

    @pl.when(z > 0)
    def _():
        gate_copy().wait_send()

    bias_pair().wait_send()
    each(1, Q, lambda k: bias_q(k).wait_send())
    each(1, T, lambda k: bias_z(k).wait_send())
    for a in range(3):
        pair_copy(a).wait_send()
        each(1, Q, lambda k: xy_copy(a, k).wait_send())
    for a in range(3):
        each(1, T, lambda k: if_duty(a, k, lambda: z_copy(a, k).wait_send()))

        def gathered():
            each(1, T, lambda k: gather_z(a, k).wait_send())

        if_duty(a, 0, gathered)

        def passed_on(kz):
            def sent():
                each(1, Q, lambda k: gather_q(a, kz, k).wait_send())

            if_duty(a, -kz, sent)

        each(0, T, passed_on)
        each(0, Q, lambda k: gather_pair(a, k).wait_send())


def finish_body(
    D, R, scale, act, igrad, total, bgrad, act_out, igrad_out, kernel_out, bias_out,
    kernel_grad, bias_grad, sem,
):
    rows = kernel_grad.shape[1]
    copies = [
        pltpu.make_async_copy(act, act_out, sem.at[0]),
        pltpu.make_async_copy(igrad, igrad_out, sem.at[1]),
        pltpu.make_async_copy(bias_grad, bias_out, sem.at[2]),
    ]
    copies[0].start()
    copies[1].start()
    bias_grad[...] = bgrad[...] * scale
    copies[2].start()
    for a in range(3):
        for b in range(pl.cdiv(rows, R)):
            n = min(R, rows - b * R)
            kernel_grad[a, b * R : b * R + n] = total[b, a, 0:n].astype(F32) * scale
        copies.append(pltpu.make_async_copy(kernel_grad.at[a], kernel_out.at[a], sem.at[3 + a]))
        copies[-1].start()
    for copy in copies:
        copy.wait()


def body(T, D, loaded, frame_index, out_grad, kernel, conv_bias):
    _, F, H, W, C = loaded.shape
    Q = D // 2
    K3, HW = 3 * C, H * W
    R = 16 * pl.cdiv(pl.cdiv(3 * K3, 16), D)
    U = 16 * pl.cdiv(R // 16, T)
    pieces = pl.cdiv(R, U)
    dims = (T, D, F, H, W, C, R, U, pieces)
    vmem = pl.BlockSpec(memory_space=pltpu.VMEM)
    hbm = pl.BlockSpec(memory_space=pltpu.HBM)
    V = pltpu.VMEM
    S = pltpu.SemaphoreType.DMA
    act, igrad, total, bgrad = pl.pallas_call(
        functools.partial(kernel_body, dims),
        out_shape=(
            jax.ShapeDtypeStruct((F, H, W, C), BF16),
            jax.ShapeDtypeStruct((F, H, W, C), BF16),
            jax.ShapeDtypeStruct((D, 3, pieces * U, C), BF16),
            jax.ShapeDtypeStruct((1, C), F32),
        ),
        in_specs=[hbm] * 5,
        out_specs=(vmem, vmem, vmem, vmem),
        scratch_shapes=[
            pltpu.SMEM((1, F), jnp.int32), V((F, H, W, C), BF16), V((1, C), F32),
            V((F, H, W, C), BF16), V((9, K3, C), BF16), V((9, K3, C), BF16),
            V((T, CAP * H + 1, W, C), BF16), V((T, CAP * H + 1, W, C), BF16),
            V((F + 6, H, W, C), BF16),
            V((F + 2, H + 2, W, K3), BF16), V((K3, (F + 2) * HW), BF16),
            V((F + 2, H + 2, W, K3), BF16),
            V((3, D * R, C), F32), V((3, D * R, C), BF16),
            V((3, Q * R, C), BF16), V((3, Q * R, C), F32), V((3, Q * R, C), BF16),
            V((3, Q, R, C), BF16), V((3, pieces * U, C), F32), V((3, pieces * U, C), BF16),
            V((3, T, U, C), BF16),
            V((8, C), F32), V((8, C), F32), V((Q, 8, C), F32), V((T, 8, C), F32),
            S((5,)), S((T,)), S((T,)), S, S, S, S,
            S((3,)), S((3,)), S((3, Q)), S((3, Q)), S((3, T)), S((3, T)),
            S((3, T)), S((3, T)), S((3, T, Q)), S((3, T, Q)), S((3, Q)), S((3, Q)),
            S, S, S((Q,)), S((Q,)), S((T,)), S((T,)),
        ],
        compiler_params=pltpu.CompilerParams(
            collective_id=0, has_side_effects=True, vmem_limit_bytes=48 * 1024 * 1024
        ),
    )(*(
        pltpu.with_memory_space_constraint(x, pltpu.HBM)
        for x in (frame_index, loaded[0], out_grad[0], kernel.reshape(9, K3, C), conv_bias[None])
    ))
    scale = 1.0 / math.sqrt(T * F * HW * D * loaded.shape[0])
    act, igrad, kernel_grad, bias_grad = pl.pallas_call(
        functools.partial(finish_body, D, R, scale),
        out_shape=(
            jax.ShapeDtypeStruct((F, H, W, C), BF16),
            jax.ShapeDtypeStruct((F, H, W, C), BF16),
            jax.ShapeDtypeStruct((3, 3 * K3, C), F32),
            jax.ShapeDtypeStruct((1, C), F32),
        ),
        in_specs=[vmem] * 4,
        out_specs=[hbm] * 4,
        scratch_shapes=[V((3, 3 * K3, C), F32), V((1, C), F32), S((6,))],
        compiler_params=pltpu.CompilerParams(vmem_limit_bytes=8 * 1024 * 1024),
    )(act, igrad, total, bgrad)
    return act[None], igrad[None], kernel_grad.reshape(kernel.shape), bias_grad[0]


def solution(mesh):
    spread = P("dp", "tm", None, None, None)
    return jax.shard_map(
        functools.partial(body, mesh.shape["tm"], mesh.shape["dp"]),
        mesh=mesh,
        in_specs=(spread, P("dp", "tm"), spread, P(), P()),
        out_specs=(spread, spread, P(), P()),
        check_vma=False,
    )
```
